32 devices in a mesh: expert: 8 (over z, x), shard: 4 (over y, core).
Axes of the slice: x: 2, y: 2, z: 4, core: 2. Of those that a mesh axis runs over, the one named last changes fastest.
Arguments:
- block_in: bfloat16 [1024, 768], P('expert'), may hold values from -6 to 6
- qkv_weight: bfloat16 [3, 768, 768], P(None, 'expert', 'shard'), may hold values from -0.21875 to 0.21875
- out_weight: bfloat16 [768, 768], P('expert', 'shard'), may hold values from -1.25 to 1.25
- norm1_gain: bfloat16 [768], P('expert'), may hold values from 0.099609375 to 1.8984375
- norm2_gain: bfloat16 [768], P('expert'), may hold values from 0.099609375 to 1.8984375
- router_weight: bfloat16 [768, 8], P('expert'), may hold values from -0.4375 to 0.4375
- rel_bias: float32 [32, 12], P(None, 'shard'), may hold values from -4 to 4
- expert_in: bfloat16 [8, 768, 3072], P('expert', None, 'shard'), may hold values from -0.21875 to 0.21875
- expert_out: bfloat16 [8, 3072, 768], P('expert', 'shard'), may hold values from -0.109375 to 0.109375
- routes: int32 [1024, 2], P('expert'), may hold values from 0 to 7, all different within a row; in each aligned block of 128 rows (0 to 127, 128 to 255, ...) at most 64 rows name the same one
- cotangent: bfloat16 [1024, 768], P('expert'), may hold values from -6 to 6
Outputs:
- block_out: bfloat16 [1024, 768], P('expert')
- input_grad: float32 [1024, 768], P('expert')
- qkv_grad: float32 [3, 768, 768], P(None, 'expert', 'shard')
- out_grad: float32 [768, 768], P('expert', 'shard')
- norm1_grad: float32 [768], P('expert')
- norm2_grad: float32 [768], P('expert')
- router_grad: float32 [768, 8], P('expert')
- bias_grad: float32 [32, 12], P(None, 'shard')
- expert_in_grad: float32 [8, 768, 3072], P('expert', None, 'shard')
- expert_out_grad: float32 [8, 3072, 768], P('expert', 'shard')
The draws below stay inside these ranges and needn't reach their ends.
Inputs may be any that keep to these rules, and one draw needn't show every extreme that they name: `routes`: the two experts of a token differ. In each aligned block of 128 rows (the rows of one sequence), no expert is named by more than 64 rows, a bound that some block reaches.
All inputs are finite; a program needn't handle non-finite values.
Results may differ from the reference program's by a relative error of at most 0.012.
The reference program's roundings to bfloat16 on the way count: a program that leaves them out, or rounds other values in their place, can miss the bound.
Values may be sent and summed in bfloat16 or wider, within the bound.
A program may use at most 64 MiB of HBM per device.

```python
import math
import jax
import jax.numpy as jnp
import numpy as np
from jax import lax

D = 768
HEADS = 12
HEAD_DIM = 64
FF = 3072
BUCKETS = 32
MAX_DIST = 128
TOK_DEV = 128
EXPERTS = 8
TOKENS = 1024
CAP = 64


def strengthened(values, key, source, target, parts, factor):
    def block_of(dim):
        return (jnp.arange(values.shape[dim]) // (values.shape[dim] // parts)).reshape((-1,) + (1,) * (values.ndim - 1 - dim))

    near = jax.random.permutation(key, parts)[block_of(target)]
    second = (block_of(target) + parts // 2) % parts
    return jnp.where((block_of(source) == near) | (block_of(source) == second), factor * values, values)


def steps_of(rng, shape, cuts, least, high):
    loudness = 1.0
    for position, shards_of in cuts:
        draws = jax.random.uniform(jax.random.fold_in(jax.random.fold_in(rng, 6), position), (shards_of,), jnp.float32, least / len(cuts), high / len(cuts))
        loudness = loudness * jnp.repeat(jnp.exp(draws), shape[position] // shards_of).reshape((-1,) + (1,) * (len(shape) - 1 - position))
    return loudness


def assign_block(own_key, own, number, rows, number_of, top, most, slope):
    ranking = jax.random.permutation(own_key, number_of)
    crowded, usual = load_shares(number_of, rows * top, most, slope, True), load_shares(number_of, rows * top, most, slope, False)
    places = jnp.arange(number_of)

    def named(lengths, turn):
        used = int((lengths > 0).sum())
        fixed = max(1, used // 4)
        shifted = fixed + (places - fixed + turn * (used - fixed)) % max(1, number_of - fixed)
        return jnp.zeros((number_of,), jnp.int32).at[ranking[jnp.where(places < fixed, places, shifted)]].set(jnp.asarray(lengths, jnp.int32))

    lengths = jnp.where(number % 4 == 0, named(crowded, number // 4), named(usual, number - number // 4 - 1))
    mixed = jax.random.permutation(jax.random.fold_in(own, 3), number_of)
    donor, receiver = mixed[0:number_of // 2 * 2:2], mixed[1:number_of // 2 * 2:2]
    slack = jnp.minimum(lengths[donor] - 1, most - lengths[receiver]) // 2
    slack = jnp.where((donor == ranking[0]) | (receiver == ranking[0]) | (lengths[receiver] == 0), 0, jnp.maximum(slack, 0))
    shifted = jax.random.randint(jax.random.fold_in(own, 4), (number_of // 2,), 0, 1 << 20) % (slack + 1)
    lengths = lengths.at[donor].add(-shifted).at[receiver].add(shifted)
    items = jnp.searchsorted(jnp.cumsum(lengths), jnp.arange(rows * top), side="right").astype(jnp.int32)
    table = items.reshape(top, rows).T
    table = table[jax.random.permutation(jax.random.fold_in(own, 1), rows)]
    turn = jax.random.randint(jax.random.fold_in(own, 2), (rows, 1), 0, top)
    return jnp.take_along_axis(table, (jnp.arange(top)[None, :] + turn) % top, axis=1)


def load_shares(amount, total, bound, lean, full):
    portions = [(1 << 20) // math.isqrt(rank ** lean) + 1 for rank in range(1, amount + 1)]
    largest = bound if full else min(bound, max(-(-total // amount), total * portions[0] // sum(portions)))
    least = 1 if total - largest >= amount - 1 else 0
    counts, spare = [largest] + [least] * (amount - 1), total - largest - least * (amount - 1)
    while spare > 0:
        movable = [i for i in range(1, amount) if counts[i] < largest] or [i for i in range(1, amount) if counts[i] < bound]
        pool, budget = sum([portions[i] for i in movable]), spare
        for i in movable:
            more = min(bound - counts[i], max(1, budget * portions[i] // pool), spare)
            counts[i] = counts[i] + more
            spare = spare - more
    return np.array(counts)


def scatter_about(key, dims, deviation, bound, cuts=(), kind=jnp.bfloat16):
    values = deviation * jax.random.normal(key, dims, jnp.float32)
    if cuts:
        values = values * steps_of(key, dims, cuts, -0.22, 0.18)
    return jnp.clip(values, -bound, bound).astype(kind)


def gaussian_with(own_key, extent, spread, most, cuts, heavy, held_as=jnp.bfloat16):
    drawn = spread * jax.random.normal(own_key, extent, jnp.float32)
    if cuts:
        drawn = drawn * steps_of(own_key, extent, cuts, -0.22, 0.18)
    return jnp.clip(strengthened(drawn, jax.random.fold_in(own_key, 3), *heavy), -most, most).astype(held_as)


def setup_inputs(seed: int = 0) -> dict:
    seeds = jax.random.split(jax.random.key(seed), 12)
    block_in = gaussian_with(seeds[0], (TOKENS, D), 1.0, 6.0, ((0, 8),), (0, 1, 8, 2.0))
    qkv_weight = scatter_about(seeds[1], (3, D, D), D ** -0.5, 0.21875, ((1, 8), (2, 4)))
    out_weight = scatter_about(seeds[2], (D, D), (D // 32) ** -0.5, 1.25, ((0, 8), (1, 4)))
    norm1_gain = jnp.clip(1.0 + 0.18 * jax.random.normal(seeds[3], (D,), jnp.float32), 0.099609375, 1.8984375).astype(jnp.bfloat16)
    norm2_gain = jnp.clip(1.0 + 0.18 * jax.random.normal(seeds[4], (D,), jnp.float32), 0.099609375, 1.8984375).astype(jnp.bfloat16)
    router_weight = scatter_about(seeds[5], (D, EXPERTS), (D // 4) ** -0.5, 0.4375, ((0, 8),))
    rel_bias = scatter_about(seeds[6], (BUCKETS, HEADS), 1.0, 4.0, ((1, 4),), jnp.float32)
    expert_in = scatter_about(seeds[7], (EXPERTS, D, FF), D ** -0.5, 0.21875, ((0, 8), (2, 4)))
    expert_out = scatter_about(seeds[8], (EXPERTS, FF, D), FF ** -0.5, 0.109375, ((0, 8), (1, 4)))
    routes_keys = jax.random.split(jax.random.fold_in(seeds[9], 1), TOKENS // TOK_DEV)
    routes_turns = jax.random.permutation(jax.random.fold_in(seeds[9], 3), TOKENS // TOK_DEV)
    routes = jax.vmap(lambda own, number: assign_block(jax.random.fold_in(seeds[9], 2), own, number, TOK_DEV, EXPERTS, 2, CAP, 2))(routes_keys, routes_turns).reshape((TOKENS, 2))
    cotangent = gaussian_with(seeds[10], (TOKENS, D), 1.0, 6.0, ((0, 8),), (0, 1, 8, 2.0))
    return dict(block_in=block_in, qkv_weight=qkv_weight, out_weight=out_weight, norm1_gain=norm1_gain, norm2_gain=norm2_gain, router_weight=router_weight, rel_bias=rel_bias, expert_in=expert_in, expert_out=expert_out, routes=routes, cotangent=cotangent)


EPS = 1e-06

def bucket_edges():
    exact_count = BUCKETS // 2
    edge_list = []
    for bucket_id in range(1, BUCKETS):
        if bucket_id < exact_count:
            edge_list.append(bucket_id)
        else:
            edge_list.append(math.ceil(exact_count * (MAX_DIST / exact_count) ** ((bucket_id - exact_count) / (BUCKETS - exact_count))))
    return jnp.array(edge_list, dtype=jnp.int32)

def gelu_parts(pre_act):
    cumulative = 0.5 * (1.0 + jax.scipy.special.erf(pre_act * (1.0 / math.sqrt(2.0))))
    density = jnp.exp(-0.5 * pre_act * pre_act) * (1.0 / math.sqrt(2.0 * math.pi))
    return (pre_act * cumulative, cumulative + pre_act * density)

def normalize(matrix):
    inverse = lax.rsqrt(lax.optimization_barrier(jnp.mean(matrix * matrix, axis=-1, keepdims=True)) + EPS)
    return (matrix * inverse, inverse)

def norm_back(upstream, normed, inverse, gain_vector):
    scaled = upstream * gain_vector
    return inverse * (scaled - normed * lax.optimization_barrier(jnp.mean(scaled * normed, axis=-1, keepdims=True)))

def reference(block_in, qkv_weight, out_weight, norm1_gain, norm2_gain, router_weight, rel_bias, expert_in, expert_out, routes, cotangent):
    seq_count = TOKENS // TOK_DEV
    score_scale = 1.0 / math.sqrt(HEAD_DIM)
    positions = jnp.arange(TOK_DEV, dtype=jnp.int32)
    distance = jnp.maximum(positions[:, None] - positions[None, :], 0)
    bucket_map = lax.optimization_barrier(jnp.sum((distance[:, :, None] >= bucket_edges()[None, None, :]).astype(jnp.int32), axis=-1))
    bucket_flat = bucket_map.reshape(-1)
    causal = positions[:, None] >= positions[None, :]
    bias_full = jnp.transpose(rel_bias[bucket_map], (2, 0, 1))
    qkv_wide = qkv_weight.astype(jnp.float32)
    out_wide = out_weight.astype(jnp.float32)
    gain_one = norm1_gain.astype(jnp.float32)
    gain_two = norm2_gain.astype(jnp.float32)

    def split_heads(projected):
        return [projected[index_c].reshape(TOK_DEV, HEADS, HEAD_DIM).astype(jnp.float32) for index_c in range(3)]

    def attention_scores(queries, keys_seq):
        raw_scores = jnp.einsum('ihd,jhd->hij', queries, keys_seq) * score_scale + bias_full
        return jnp.where(causal[None], raw_scores, -jnp.inf)

    def forward_seq(carry, seq_in):
        inputs = seq_in.astype(jnp.float32)
        normed_one, inverse_one = normalize(inputs)
        hidden_one = (normed_one * gain_one).astype(jnp.bfloat16)
        projected = jnp.einsum('td,cdj->ctj', hidden_one.astype(jnp.float32), qkv_wide).astype(jnp.bfloat16)
        queries, keys_seq, values_seq = split_heads(projected)
        scores = attention_scores(queries, keys_seq)
        log_total = jnp.log(lax.optimization_barrier(jnp.sum(jnp.exp(scores), axis=-1)))
        attention_low = jnp.exp(scores - log_total[..., None]).astype(jnp.bfloat16)
        attended = jnp.einsum('hij,jhd->ihd', attention_low.astype(jnp.float32), values_seq).astype(jnp.bfloat16).reshape(TOK_DEV, D)
        mixed = jnp.einsum('tc,mc->tm', attended.astype(jnp.float32), out_wide)
        return (carry, (inputs + mixed, normed_one, inverse_one, hidden_one, projected, log_total, attended))
    _, saved = lax.scan(forward_seq, jnp.zeros((), jnp.float32), block_in.reshape(seq_count, TOK_DEV, D))
    residual_one = saved[0].reshape(TOKENS, D)
    normed_two, inverse_two = normalize(residual_one)
    hidden_two = (normed_two * gain_two).astype(jnp.bfloat16)
    logits = jnp.dot(hidden_two, router_weight, preferred_element_type=jnp.float32)
    chosen = jnp.take_along_axis(logits, routes, axis=1)
    chosen_exp = jnp.exp(chosen)
    gate_value = chosen_exp / lax.optimization_barrier(jnp.sum(chosen_exp, axis=1, keepdims=True))
    pair_routes = routes.reshape(seq_count, 2 * TOK_DEV)
    counts_hot = (pair_routes[:, :, None] == jnp.arange(EXPERTS, dtype=jnp.int32)[None, None, :]).astype(jnp.int32)
    slot_index = lax.optimization_barrier(jnp.sum((jnp.cumsum(counts_hot, axis=1) - 1) * counts_hot, axis=-1))
    seq_ids = jnp.arange(seq_count, dtype=jnp.int32)[:, None]
    slot_target = ((pair_routes * seq_count + seq_ids) * CAP + slot_index).reshape(-1).astype(jnp.int32)
    total_slots = EXPERTS * seq_count * CAP
    pair_rows = jnp.repeat(hidden_two, 2, axis=0)
    slot_buffer = jnp.zeros((total_slots, D), jnp.bfloat16).at[slot_target].set(pair_rows).reshape(EXPERTS, seq_count * CAP, D)

    def expert_forward(items):
        slot_rows, weight_in, weight_out = items
        pre_act = jnp.dot(slot_rows, weight_in, preferred_element_type=jnp.float32)
        activated, _ = gelu_parts(pre_act)
        return jnp.dot(activated.astype(jnp.bfloat16), weight_out, preferred_element_type=jnp.float32).astype(jnp.bfloat16)
    expert_rows = lax.map(expert_forward, (slot_buffer, expert_in, expert_out))
    returned = expert_rows.reshape(total_slots, D)[slot_target].reshape(TOKENS, 2, D)
    mixture = lax.optimization_barrier(jnp.sum(gate_value[:, :, None] * returned.astype(jnp.float32), axis=1))
    block_out = (residual_one + mixture).astype(jnp.bfloat16)
    upstream = cotangent.astype(jnp.float32)
    gate_grad = lax.optimization_barrier(jnp.sum(upstream[:, None, :] * returned.astype(jnp.float32), axis=-1))
    logit_pair = gate_value * (gate_grad - lax.optimization_barrier(jnp.sum(gate_value * gate_grad, axis=1, keepdims=True)))
    token_ids = jnp.arange(TOKENS, dtype=jnp.int32)
    logit_grad = jnp.zeros((TOKENS, EXPERTS), jnp.float32).at[token_ids[:, None], routes].add(logit_pair).astype(jnp.bfloat16)
    router_grad = jnp.dot(hidden_two.T, logit_grad, preferred_element_type=jnp.float32)
    from_router = jnp.dot(logit_grad, router_weight.T, preferred_element_type=jnp.float32)
    slot_grad_rows = (gate_value[:, :, None] * upstream[:, None, :]).astype(jnp.bfloat16).reshape(2 * TOKENS, D)
    grad_buffer = jnp.zeros((total_slots, D), jnp.bfloat16).at[slot_target].set(slot_grad_rows).reshape(EXPERTS, seq_count * CAP, D)

    def expert_backward(items):
        slot_rows, slot_grad, weight_in, weight_out = items
        pre_act = jnp.dot(slot_rows, weight_in, preferred_element_type=jnp.float32)
        activated, gelu_slope = gelu_parts(pre_act)
        act_low = activated.astype(jnp.bfloat16)
        act_grad = jnp.dot(slot_grad, weight_out.T, preferred_element_type=jnp.float32)
        pre_grad = (act_grad * gelu_slope).astype(jnp.bfloat16)
        grad_in = jnp.dot(slot_rows.T, pre_grad, preferred_element_type=jnp.float32)
        grad_out = jnp.dot(act_low.T, slot_grad, preferred_element_type=jnp.float32)
        row_back = jnp.dot(pre_grad, weight_in.T, preferred_element_type=jnp.float32).astype(jnp.bfloat16)
        return (grad_in, grad_out, row_back)
    expert_in_grad, expert_out_grad, row_back = lax.map(expert_backward, (slot_buffer, grad_buffer, expert_in, expert_out))
    row_grad = row_back.reshape(total_slots, D)[slot_target].reshape(TOKENS, 2, D)
    hidden_two_grad = lax.optimization_barrier(jnp.sum(row_grad.astype(jnp.float32), axis=1)) + from_router
    norm2_grad = lax.optimization_barrier(jnp.sum(hidden_two_grad * normed_two, axis=0))
    residual_grad = upstream + norm_back(hidden_two_grad, normed_two, inverse_two, gain_two)

    def backward_seq(carry, items):
        qkv_acc, out_acc, gain_acc, bias_acc = carry
        grad_seq, normed_one, inverse_one, hidden_one, projected, log_total, attended = items
        queries, keys_seq, values_seq = split_heads(projected)
        scores = attention_scores(queries, keys_seq)
        attention = jnp.exp(scores - log_total[..., None])
        attention_low = attention.astype(jnp.bfloat16)
        grad_low = grad_seq.astype(jnp.bfloat16)
        out_part = jnp.einsum('tm,tc->mc', grad_low.astype(jnp.float32), attended.astype(jnp.float32))
        attended_grad = jnp.einsum('tm,mc->tc', grad_low.astype(jnp.float32), out_wide).astype(jnp.bfloat16).reshape(TOK_DEV, HEADS, HEAD_DIM)
        value_grad = jnp.einsum('hij,ihd->jhd', attention_low.astype(jnp.float32), attended_grad.astype(jnp.float32))
        prob_grad = jnp.einsum('ihd,jhd->hij', attended_grad.astype(jnp.float32), values_seq)
        row_delta = lax.optimization_barrier(jnp.sum(attended_grad.astype(jnp.float32) * attended.reshape(TOK_DEV, HEADS, HEAD_DIM).astype(jnp.float32), axis=-1)).T
        score_grad = attention * (prob_grad - row_delta[:, :, None])
        bias_part = jax.ops.segment_sum(jnp.transpose(score_grad, (1, 2, 0)).reshape(TOK_DEV * TOK_DEV, HEADS), bucket_flat, num_segments=BUCKETS)
        score_low = score_grad.astype(jnp.bfloat16).astype(jnp.float32)
        query_grad = (jnp.einsum('hij,jhd->ihd', score_low, keys_seq) * score_scale).astype(jnp.bfloat16)
        key_grad = (jnp.einsum('hij,ihd->jhd', score_low, queries) * score_scale).astype(jnp.bfloat16)
        stacked = jnp.stack([query_grad, key_grad, value_grad.astype(jnp.bfloat16)]).reshape(3, TOK_DEV, D).astype(jnp.float32)
        qkv_part = jnp.einsum('td,ctj->cdj', hidden_one.astype(jnp.float32), stacked)
        hidden_one_grad = jnp.einsum('ctj,cdj->td', stacked, qkv_wide)
        gain_part = lax.optimization_barrier(jnp.sum(hidden_one_grad * normed_one, axis=0))
        input_seq = grad_seq + norm_back(hidden_one_grad, normed_one, inverse_one, gain_one)
        return ((qkv_acc + qkv_part, out_acc + out_part, gain_acc + gain_part, bias_acc + bias_part), input_seq)
    start = (jnp.zeros((3, D, D), jnp.float32), jnp.zeros((D, D), jnp.float32), jnp.zeros((D,), jnp.float32), jnp.zeros((BUCKETS, HEADS), jnp.float32))
    seq_items = (residual_grad.reshape(seq_count, TOK_DEV, D),) + tuple(saved[1:])
    sums, input_seqs = lax.scan(backward_seq, start, seq_items)
    qkv_grad, out_grad, norm1_grad, bias_grad = sums
    input_grad = input_seqs.reshape(TOKENS, D)
    return (block_out, input_grad, qkv_grad, out_grad, norm1_grad, norm2_grad, router_grad, bias_grad, expert_in_grad, expert_out_grad)
```

```python
import math

import jax
import jax.numpy as jnp
from jax import lax
from jax.experimental import pallas as pl
from jax.experimental.pallas import tpu as pltpu
from jax.sharding import PartitionSpec as P

HEAD_DIM = 64
BUCKETS = 32
MAX_DIST = 128


EPS = 1e-06


def bucket_edges():
    exact_count = BUCKETS // 2
    edge_list = []
    for bucket_id in range(1, BUCKETS):
        if bucket_id < exact_count:
            edge_list.append(bucket_id)
        else:
            edge_list.append(
                math.ceil(
                    exact_count
                    * (MAX_DIST / exact_count)
                    ** ((bucket_id - exact_count) / (BUCKETS - exact_count))
                )
            )
    return jnp.array(edge_list, dtype=jnp.int32)


def bucket_onehot(length):
    distance = lax.broadcasted_iota(jnp.int32, (length, 1), 0)
    bucket = jnp.sum((distance >= bucket_edges()[None, :]).astype(jnp.int32), axis=1)
    return (bucket[:, None] == lax.broadcasted_iota(jnp.int32, (length, BUCKETS), 1)).astype(
        jnp.float32
    )


def toeplitz(per_distance):
    head_count, length = per_distance.shape
    widened = jnp.concatenate(
        [jnp.zeros((head_count, length - 1), per_distance.dtype), per_distance], axis=1
    )
    rows_flat = jnp.broadcast_to(widened[:, None, :], (head_count, length, 2 * length - 1)).reshape(
        head_count, -1
    )
    shifted = jnp.pad(rows_flat, ((0, 0), (0, length))).reshape(head_count, length, 2 * length)[
        :, :, :length
    ]
    return jnp.flip(shifted, axis=2)


def diagonal_sums(matrix):
    head_count, length, _ = matrix.shape
    padded = jnp.pad(jnp.flip(matrix, axis=2), ((0, 0), (0, 0), (0, length))).reshape(
        head_count, -1
    )
    skewed = padded[:, : length * (2 * length - 1)].reshape(head_count, length, 2 * length - 1)
    return jnp.sum(skewed, axis=1)[:, length - 1 :]


def gelu_parts(pre_act):
    cumulative = 0.5 * (1.0 + jax.scipy.special.erf(pre_act * (1.0 / math.sqrt(2.0))))
    density = jnp.exp(-0.5 * pre_act * pre_act) * (1.0 / math.sqrt(2.0 * math.pi))
    return (pre_act * cumulative, cumulative + pre_act * density)


def normalize(matrix):
    inverse = lax.rsqrt(jnp.mean(matrix * matrix, axis=-1, keepdims=True) + EPS)
    return (matrix * inverse, inverse)


def norm_back(upstream, normed, inverse, gain_vector):
    scaled = upstream * gain_vector
    return inverse * (scaled - normed * jnp.mean(scaled * normed, axis=-1, keepdims=True))


MESH = pl.DeviceIdType.MESH
DMA = pltpu.SemaphoreType.DMA


def remote(source, target, sent, arrived, axis, peer):
    return pltpu.make_async_remote_copy(
        src_ref=source,
        dst_ref=target,
        send_sem=sent,
        recv_sem=arrived,
        device_id={axis: peer},
        device_id_type=MESH,
    )


def greet(axis_peers):
    barrier = pltpu.get_barrier_semaphore()
    for axis, peer in axis_peers:
        pl.semaphore_signal(barrier, inc=1, device_id={axis: peer}, device_id_type=MESH)
    pl.semaphore_wait(barrier, len(axis_peers))


def call(kernel, out_shape, scratch, collective, operands):
    vmem = pl.BlockSpec(memory_space=pltpu.VMEM)
    return pl.pallas_call(
        kernel,
        out_shape=out_shape,
        in_specs=[vmem] * len(operands),
        out_specs=jax.tree.map(lambda _: vmem, out_shape),
        scratch_shapes=scratch,
        compiler_params=pltpu.CompilerParams(collective_id=collective, has_side_effects=True),
    )(*operands)


def exchange(axis, collective, spread, shared):
    count = lax.axis_size(axis)
    operands = tuple(spread) + tuple(shared)
    total = len(operands)

    def kernel(*refs):
        ins, outs = refs[:total], refs[total : 2 * total]
        sent, arrived, own_sem = refs[2 * total :]
        me = lax.axis_index(axis)
        greet([(axis, lax.rem(me + step, count)) for step in range(1, count)])
        copies = []
        for step in range(1, count):
            peer = lax.rem(me + step, count)
            for index in range(total):
                source = ins[index].at[peer] if index < len(spread) else ins[index]
                copy = remote(
                    source,
                    outs[index].at[me],
                    sent.at[index, step],
                    arrived.at[index, step],
                    axis,
                    peer,
                )
                copy.start()
                copies.append(copy)
        for index in range(total):
            source = ins[index].at[me] if index < len(spread) else ins[index]
            copy = pltpu.make_async_copy(source, outs[index].at[me], own_sem.at[index])
            copy.start()
            copies.append(copy)
        for copy in copies:
            copy.wait()

    out_shape = [jax.ShapeDtypeStruct(x.shape, x.dtype) for x in spread] + [
        jax.ShapeDtypeStruct((count,) + x.shape, x.dtype) for x in shared
    ]
    scratch = [DMA((total, count)), DMA((total, count)), DMA((total,))]
    return call(kernel, out_shape, scratch, collective, operands)


def square(shard):
    beside = shard + 1 - 2 * lax.rem(shard, 2)
    across = lax.rem(shard + 2, 4)
    return beside, across, lax.rem(beside + 2, 4)


def dispatch(buffer, collective):
    experts, capacity, width = buffer.shape

    def kernel(in_ref, out_ref, sent, arrived, own_sem):
        me, shard = lax.axis_index("expert"), lax.axis_index("shard")
        beside, across, _ = square(shard)
        greet(
            [("expert", lax.rem(me + step, experts)) for step in range(1, experts)]
            + [("shard", beside), ("shard", across)]
        )
        first = []
        for step in range(1, experts):
            peer = lax.rem(me + step, experts)
            copy = remote(
                in_ref.at[peer],
                out_ref.at[shard, me],
                sent.at[0, step],
                arrived.at[0, step],
                "expert",
                peer,
            )
            copy.start()
            first.append(copy)
        own = pltpu.make_async_copy(in_ref.at[me], out_ref.at[shard, me], own_sem)
        own.start()
        near, far, last = [], [], []
        for step in range(experts):
            origin = lax.rem(me + experts - step, experts)
            if step:
                first[step - 1].wait_recv()
            else:
                own.wait()
            block = out_ref.at[shard, origin]
            copy = remote(block, block, sent.at[2, step], arrived.at[2, step], "shard", across)
            copy.start()
            far.append(copy)
            copy = remote(block, block, sent.at[1, step], arrived.at[1, step], "shard", beside)
            copy.start()
            near.append(copy)
        for step in range(experts):
            origin = lax.rem(me + experts - step, experts)
            far[step].wait_recv()
            block = out_ref.at[across, origin]
            copy = remote(block, block, sent.at[3, step], arrived.at[3, step], "shard", beside)
            copy.start()
            last.append(copy)
        for copy in first + far:
            copy.wait_send()
        for copy in near + last:
            copy.wait()

    return call(
        kernel,
        jax.ShapeDtypeStruct((4, experts, capacity, width), buffer.dtype),
        [DMA((4, experts)), DMA((4, experts)), DMA],
        collective,
        (buffer,),
    )


def give_back(parts, collective):
    _, experts, capacity, width = parts.shape
    block_shape = (experts, capacity, width)

    def kernel(in_ref, out_ref, pair, own_sum, send_sum, far_sum, ready, sent, arrived, own_sem):
        me, shard = lax.axis_index("expert"), lax.axis_index("shard")
        beside, across, corner = square(shard)
        greet(
            [("expert", lax.rem(me + step, experts)) for step in range(1, experts)]
            + [("shard", beside), ("shard", across)]
        )
        near, far, last = [], [], []
        for step in range(experts):
            peer = lax.rem(me + step + 1, experts)
            for which, quarter in ((0, corner), (1, beside)):
                copy = remote(
                    in_ref.at[quarter, peer],
                    pair.at[which, step],
                    sent.at[which, step],
                    arrived.at[which, step],
                    "shard",
                    beside,
                )
                copy.start()
                near.append(copy)
        for step in range(experts):
            peer = lax.rem(me + step + 1, experts)
            near[2 * step].wait_recv()
            send_sum[step] = (
                in_ref[across, peer].astype(jnp.float32) + pair[0, step].astype(jnp.float32)
            ).astype(jnp.bfloat16)
            copy = remote(
                send_sum.at[step],
                far_sum.at[step],
                sent.at[2, step],
                arrived.at[2, step],
                "shard",
                across,
            )
            copy.start()
            far.append(copy)
            near[2 * step + 1].wait_recv()
            own_sum[step] = in_ref[shard, peer].astype(jnp.float32) + pair[1, step].astype(
                jnp.float32
            )
        for step in range(experts):
            peer = lax.rem(me + step + 1, experts)
            far[step].wait_recv()
            ready[step] = (own_sum[step] + far_sum[step].astype(jnp.float32)).astype(jnp.bfloat16)
            if step < experts - 1:
                copy = remote(
                    ready.at[step],
                    out_ref.at[me],
                    sent.at[3, step],
                    arrived.at[3, step],
                    "expert",
                    peer,
                )
            else:
                copy = pltpu.make_async_copy(ready.at[step], out_ref.at[me], own_sem)
            copy.start()
            last.append(copy)
        for copy in near + far:
            copy.wait_send()
        for copy in last:
            copy.wait()

    return call(
        kernel,
        jax.ShapeDtypeStruct(block_shape, jnp.bfloat16),
        [
            pltpu.VMEM((2,) + block_shape, jnp.bfloat16),
            pltpu.VMEM(block_shape, jnp.float32),
            pltpu.VMEM(block_shape, jnp.bfloat16),
            pltpu.VMEM(block_shape, jnp.bfloat16),
            pltpu.VMEM(block_shape, jnp.bfloat16),
            DMA((4, experts)),
            DMA((4, experts)),
            DMA,
        ],
        collective,
        (parts,),
    )


def sum_shards(part, collective):
    (gathered,) = exchange("shard", collective, (), (part.astype(jnp.bfloat16),))
    return jnp.sum(gathered.astype(jnp.float32), axis=0)


def local(
    block_in,
    qkv_weight,
    out_weight,
    norm1_gain,
    norm2_gain,
    router_weight,
    rel_bias,
    expert_in,
    expert_out,
    routes,
    cotangent,
):
    length, model_width = block_in.shape
    experts = lax.axis_size("expert")
    capacity = 4 * length // experts
    score_scale = 1.0 / math.sqrt(HEAD_DIM)
    shards = lax.axis_size("shard")
    shard = lax.axis_index("shard")
    quarter = model_width // shards
    small = jnp.concatenate([norm1_gain[None], norm2_gain[None], router_weight.T], axis=0)
    weights = jnp.concatenate([qkv_weight, out_weight[None]], axis=0)
    weights_all, small_all = exchange("expert", 0, (), (weights, small))
    weights_all = weights_all.transpose(1, 0, 2, 3).reshape(4, model_width, -1)
    small_all = small_all.transpose(1, 0, 2).reshape(-1, model_width)
    qkv_full, out_full = weights_all[:3], weights_all[3]
    gain_low_one, gain_low_two, router = small_all[0], small_all[1], small_all[2:].T
    gain_one = gain_low_one.astype(jnp.float32)
    gain_two = gain_low_two.astype(jnp.float32)
    inputs = block_in.astype(jnp.float32)
    normed_one, inverse_one = normalize(inputs)
    hidden_one = (normed_one * gain_one).astype(jnp.bfloat16)
    projected = jnp.einsum(
        "td,cdj->ctj", hidden_one, qkv_full, preferred_element_type=jnp.float32
    ).astype(jnp.bfloat16)
    local_width = projected.shape[2]
    local_heads = local_width // HEAD_DIM
    queries = projected[0].reshape(length, local_heads, HEAD_DIM)
    keys_local = projected[1].reshape(length, local_heads, HEAD_DIM)
    values_local = projected[2].reshape(length, local_heads, HEAD_DIM)
    onehot_bucket = bucket_onehot(length)
    per_distance = jnp.dot(onehot_bucket, rel_bias, precision=lax.Precision.HIGHEST).T
    bias_full = toeplitz(per_distance)
    causal = lax.broadcasted_iota(jnp.int32, (length, length), 0) >= lax.broadcasted_iota(
        jnp.int32, (length, length), 1
    )

    def scores_of():
        raw_scores = (
            jnp.einsum("ihd,jhd->hij", queries, keys_local, preferred_element_type=jnp.float32)
            * score_scale
            + bias_full
        )
        return jnp.where(causal[None], raw_scores, -jnp.inf)

    scores = scores_of()
    log_total = jnp.log(jnp.sum(jnp.exp(scores), axis=-1))
    attention_low = jnp.exp(scores - log_total[..., None]).astype(jnp.bfloat16)
    attended = (
        jnp.einsum("hij,jhd->ihd", attention_low, values_local, preferred_element_type=jnp.float32)
        .astype(jnp.bfloat16)
        .reshape(length, local_width)
    )
    attn_part = jnp.einsum("tc,mc->tm", attended, out_full, preferred_element_type=jnp.float32)
    residual_one = inputs + sum_shards(attn_part, 1)
    normed_two, inverse_two = normalize(residual_one)
    hidden_two = (normed_two * gain_two).astype(jnp.bfloat16)
    logits = jnp.dot(hidden_two, router, preferred_element_type=jnp.float32)
    expert_ids = lax.broadcasted_iota(jnp.int32, (1, 1, router.shape[1]), 2)
    route_hot = (routes[:, :, None] == expert_ids).astype(jnp.float32)
    chosen = jnp.sum(logits[:, None, :] * route_hot, axis=-1)
    chosen_exp = jnp.exp(chosen)
    gate_value = chosen_exp / jnp.sum(chosen_exp, axis=1, keepdims=True)
    flat_routes = routes.reshape(-1)
    counts_hot = (flat_routes[:, None] == expert_ids[0]).astype(jnp.int32)
    slot_index = jnp.sum((jnp.cumsum(counts_hot, axis=0) - 1) * counts_hot, axis=1)
    slot_target = flat_routes * capacity + slot_index
    upstream = cotangent.astype(jnp.float32)

    def my_columns(matrix):
        return lax.dynamic_slice_in_dim(matrix, shard * quarter, quarter, axis=1)

    slots = experts * capacity
    place = (
        lax.broadcasted_iota(jnp.int32, (slots, 2 * length), 0) == slot_target[None, :]
    ).astype(jnp.bfloat16)
    hidden_rows = jnp.repeat(my_columns(hidden_two), 2, axis=0)
    slot_grad = (
        (gate_value[:, :, None] * my_columns(upstream)[:, None, :])
        .astype(jnp.bfloat16)
        .reshape(2 * length, quarter)
    )
    outgoing = jnp.dot(
        place,
        jnp.concatenate([hidden_rows, slot_grad], axis=1),
        preferred_element_type=jnp.float32,
    ).astype(jnp.bfloat16)
    incoming = dispatch(outgoing.reshape(experts, capacity, 2 * quarter), 2).reshape(
        shards, slots, 2, quarter
    )
    incoming = incoming.transpose(2, 1, 0, 3).reshape(2, slots, model_width)
    arrived, arrived_grad = incoming[0], incoming[1]
    pre_act = jnp.dot(arrived, expert_in[0], preferred_element_type=jnp.float32)
    activated, gelu_slope = gelu_parts(pre_act)
    act_low = activated.astype(jnp.bfloat16)
    expert_part = jnp.dot(act_low, expert_out[0], preferred_element_type=jnp.float32)
    act_grad = jnp.einsum(
        "rd,fd->rf", arrived_grad, expert_out[0], preferred_element_type=jnp.float32
    )
    pre_grad = (act_grad * gelu_slope).astype(jnp.bfloat16)
    row_part = jnp.einsum("rf,df->rd", pre_grad, expert_in[0], preferred_element_type=jnp.float32)
    parts = jnp.stack(
        [
            expert_part.astype(jnp.bfloat16).reshape(slots, shards, quarter),
            row_part.astype(jnp.bfloat16).reshape(slots, shards, quarter),
        ],
        axis=2,
    )
    parts = parts.transpose(1, 0, 2, 3).reshape(shards, experts, capacity, 2 * quarter)
    returned = give_back(parts, 3).reshape(slots, 2 * quarter)
    rows = jnp.einsum("sp,sc->pc", place, returned, preferred_element_type=jnp.float32).reshape(
        length, 2, 2, quarter
    )
    value_rows, grad_rows = rows[:, :, 0], rows[:, :, 1]
    block_quarter = (
        my_columns(residual_one) + jnp.sum(gate_value[:, :, None] * value_rows, axis=1)
    ).astype(jnp.bfloat16)
    gate_quarter = jnp.sum(my_columns(upstream)[:, None, :] * value_rows, axis=-1)
    bundle = jnp.concatenate(
        [block_quarter, jnp.sum(grad_rows, axis=1).astype(jnp.bfloat16)], axis=1
    )
    bundle_all, gate_all = exchange("shard", 4, (), (bundle, gate_quarter.T))
    bundle_all = (
        bundle_all.reshape(shards, length, 2, quarter)
        .transpose(2, 1, 0, 3)
        .reshape(2, length, model_width)
    )
    block_out = bundle_all[0]
    gate_grad = jnp.sum(gate_all, axis=0).T
    logit_pair = gate_value * (gate_grad - jnp.sum(gate_value * gate_grad, axis=1, keepdims=True))
    logit_grad = jnp.sum(logit_pair[:, :, None] * route_hot, axis=1).astype(jnp.bfloat16)
    router_local = jnp.einsum(
        "td,te->ed", hidden_two, logit_grad, preferred_element_type=jnp.float32
    )
    from_router = jnp.einsum("te,de->td", logit_grad, router, preferred_element_type=jnp.float32)
    expert_out_local = jnp.einsum(
        "rf,rd->fd", act_low, arrived_grad, preferred_element_type=jnp.float32
    )
    expert_in_local = jnp.einsum("rd,rf->df", arrived, pre_grad, preferred_element_type=jnp.float32)
    hidden_two_grad = bundle_all[1].astype(jnp.float32) + from_router
    gain_two_grad = jnp.sum(hidden_two_grad * normed_two, axis=0)
    residual_grad = upstream + norm_back(hidden_two_grad, normed_two, inverse_two, gain_two)
    residual_low = residual_grad.astype(jnp.bfloat16)
    out_local = jnp.einsum("tm,tc->mc", residual_low, attended, preferred_element_type=jnp.float32)
    attended_grad = (
        jnp.einsum("tm,mc->tc", residual_low, out_full, preferred_element_type=jnp.float32)
        .astype(jnp.bfloat16)
        .reshape(length, local_heads, HEAD_DIM)
    )
    scores = scores_of()
    attention = jnp.exp(scores - log_total[..., None])
    attention_low = attention.astype(jnp.bfloat16)
    value_grad = jnp.einsum(
        "hij,ihd->jhd", attention_low, attended_grad, preferred_element_type=jnp.float32
    )
    prob_grad = jnp.einsum(
        "ihd,jhd->hij", attended_grad, values_local, preferred_element_type=jnp.float32
    )
    row_delta = jnp.sum(
        attended_grad.astype(jnp.float32)
        * attended.reshape(length, local_heads, HEAD_DIM).astype(jnp.float32),
        axis=-1,
    ).T
    score_grad = attention * (prob_grad - row_delta[:, :, None])
    bias_local = jnp.dot(
        onehot_bucket.T, diagonal_sums(score_grad).T, precision=lax.Precision.HIGHEST
    )
    score_low = score_grad.astype(jnp.bfloat16)
    query_grad = (
        jnp.einsum("hij,jhd->ihd", score_low, keys_local, preferred_element_type=jnp.float32)
        * score_scale
    ).astype(jnp.bfloat16)
    key_grad = (
        jnp.einsum("hij,ihd->jhd", score_low, queries, preferred_element_type=jnp.float32)
        * score_scale
    ).astype(jnp.bfloat16)
    stacked = jnp.stack([query_grad, key_grad, value_grad.astype(jnp.bfloat16)]).reshape(
        3, length, local_width
    )
    qkv_local = jnp.einsum("td,ctj->cdj", hidden_one, stacked, preferred_element_type=jnp.float32)
    hidden_one_part = jnp.einsum(
        "ctj,cdj->td", stacked, qkv_full, preferred_element_type=jnp.float32
    )
    hidden_one_grad = sum_shards(hidden_one_part, 5)
    gain_one_grad = jnp.sum(hidden_one_grad * normed_one, axis=0)
    input_grad = residual_grad + norm_back(hidden_one_grad, normed_one, inverse_one, gain_one)
    grads = jnp.concatenate([qkv_local, out_local[None]], axis=0).astype(jnp.bfloat16)
    grads = grads.reshape(4, experts, -1, local_width).transpose(1, 0, 2, 3)
    small_grads = jnp.concatenate([gain_one_grad[None], gain_two_grad[None], router_local], axis=0)
    small_grads = small_grads.reshape(small_grads.shape[0], experts, -1).transpose(1, 0, 2)
    grads_all, small_grads_all, bias_all = exchange(
        "expert", 6, (grads, small_grads), (bias_local.T,)
    )
    grads_sum = jnp.sum(grads_all.astype(jnp.float32), axis=0)
    small_sum = jnp.sum(small_grads_all, axis=0)
    qkv_grad, out_grad = grads_sum[:3], grads_sum[3]
    norm1_grad, norm2_grad, router_grad = small_sum[0], small_sum[1], small_sum[2:].T
    bias_grad = jnp.sum(bias_all, axis=0).T
    return (
        block_out,
        input_grad,
        qkv_grad,
        out_grad,
        norm1_grad,
        norm2_grad,
        router_grad,
        bias_grad,
        expert_in_local[None],
        expert_out_local[None],
    )


def solution(mesh):
    placed = (
        P("expert", None),
        P(None, "expert", "shard"),
        P("expert", "shard"),
        P("expert"),
        P("expert"),
        P("expert", None),
        P(None, "shard"),
        P("expert", None, "shard"),
        P("expert", "shard", None),
        P("expert", None),
        P("expert", None),
    )
    return jax.shard_map(
        local,
        mesh=mesh,
        in_specs=placed,
        out_specs=(
            P("expert", None),
            P("expert", None),
            P(None, "expert", "shard"),
            P("expert", "shard"),
            P("expert"),
            P("expert"),
            P("expert", None),
            P(None, "shard"),
            P("expert", None, "shard"),
            P("expert", "shard", None),
        ),
        check_vma=False,
    )
```

```python
import math

import jax
import jax.numpy as jnp
from jax import lax
from jax.experimental import pallas as pl
from jax.experimental.pallas import tpu as pltpu
from jax.sharding import PartitionSpec as P

HEAD_DIM = 64
BUCKETS = 32
MAX_DIST = 128


EPS = 1e-06


def bucket_edges():
    exact_count = BUCKETS // 2
    edge_list = []
    for bucket_id in range(1, BUCKETS):
        if bucket_id < exact_count:
            edge_list.append(bucket_id)
        else:
            edge_list.append(
                math.ceil(
                    exact_count
                    * (MAX_DIST / exact_count)
                    ** ((bucket_id - exact_count) / (BUCKETS - exact_count))
                )
            )
    return jnp.array(edge_list, dtype=jnp.int32)


def bucket_onehot(length):
    distance = lax.broadcasted_iota(jnp.int32, (length, 1), 0)
    bucket = jnp.sum((distance >= bucket_edges()[None, :]).astype(jnp.int32), axis=1)
    return (bucket[:, None] == lax.broadcasted_iota(jnp.int32, (length, BUCKETS), 1)).astype(
        jnp.float32
    )


def toeplitz(per_distance):
    head_count, length = per_distance.shape
    widened = jnp.concatenate(
        [jnp.zeros((head_count, length - 1), per_distance.dtype), per_distance], axis=1
    )
    rows_flat = jnp.broadcast_to(widened[:, None, :], (head_count, length, 2 * length - 1)).reshape(
        head_count, -1
    )
    shifted = jnp.pad(rows_flat, ((0, 0), (0, length))).reshape(head_count, length, 2 * length)[
        :, :, :length
    ]
    return jnp.flip(shifted, axis=2)


def diagonal_sums(matrix):
    head_count, length, _ = matrix.shape
    padded = jnp.pad(jnp.flip(matrix, axis=2), ((0, 0), (0, 0), (0, length))).reshape(
        head_count, -1
    )
    skewed = padded[:, : length * (2 * length - 1)].reshape(head_count, length, 2 * length - 1)
    return jnp.sum(skewed, axis=1)[:, length - 1 :]


def gelu_parts(pre_act):
    cumulative = 0.5 * (1.0 + jax.scipy.special.erf(pre_act * (1.0 / math.sqrt(2.0))))
    density = jnp.exp(-0.5 * pre_act * pre_act) * (1.0 / math.sqrt(2.0 * math.pi))
    return (pre_act * cumulative, cumulative + pre_act * density)


def normalize(matrix):
    inverse = lax.rsqrt(jnp.mean(matrix * matrix, axis=-1, keepdims=True) + EPS)
    return (matrix * inverse, inverse)


def norm_back(upstream, normed, inverse, gain_vector):
    scaled = upstream * gain_vector
    return inverse * (scaled - normed * jnp.mean(scaled * normed, axis=-1, keepdims=True))


MESH = pl.DeviceIdType.MESH
DMA = pltpu.SemaphoreType.DMA


def remote(source, target, sent, arrived, axis, peer):
    return pltpu.make_async_remote_copy(
        src_ref=source,
        dst_ref=target,
        send_sem=sent,
        recv_sem=arrived,
        device_id={axis: peer},
        device_id_type=MESH,
    )


def greet(axis_peers):
    barrier = pltpu.get_barrier_semaphore()
    for axis, peer in axis_peers:
        pl.semaphore_signal(barrier, inc=1, device_id={axis: peer}, device_id_type=MESH)
    pl.semaphore_wait(barrier, len(axis_peers))


def call(kernel, out_shape, scratch, collective, operands):
    vmem = pl.BlockSpec(memory_space=pltpu.VMEM)
    return pl.pallas_call(
        kernel,
        out_shape=out_shape,
        in_specs=[vmem] * len(operands),
        out_specs=jax.tree.map(lambda _: vmem, out_shape),
        scratch_shapes=scratch,
        compiler_params=pltpu.CompilerParams(collective_id=collective, has_side_effects=True),
    )(*operands)


def exchange(axis, collective, spread, shared):
    count = lax.axis_size(axis)
    operands = tuple(spread) + tuple(shared)
    total = len(operands)

    def kernel(*refs):
        ins, outs = refs[:total], refs[total : 2 * total]
        sent, arrived, own_sem = refs[2 * total :]
        me = lax.axis_index(axis)
        greet([(axis, lax.rem(me + step, count)) for step in range(1, count)])
        copies = []
        for step in range(1, count):
            peer = lax.rem(me + step, count)
            for index in range(total):
                source = ins[index].at[peer] if index < len(spread) else ins[index]
                copy = remote(
                    source,
                    outs[index].at[me],
                    sent.at[index, step],
                    arrived.at[index, step],
                    axis,
                    peer,
                )
                copy.start()
                copies.append(copy)
        for index in range(total):
            source = ins[index].at[me] if index < len(spread) else ins[index]
            copy = pltpu.make_async_copy(source, outs[index].at[me], own_sem.at[index])
            copy.start()
            copies.append(copy)
        for copy in copies:
            copy.wait()

    out_shape = [jax.ShapeDtypeStruct(x.shape, x.dtype) for x in spread] + [
        jax.ShapeDtypeStruct((count,) + x.shape, x.dtype) for x in shared
    ]
    scratch = [DMA((total, count)), DMA((total, count)), DMA((total,))]
    return call(kernel, out_shape, scratch, collective, operands)


def square(shard):
    beside = shard + 1 - 2 * lax.rem(shard, 2)
    across = lax.rem(shard + 2, 4)
    return beside, across, lax.rem(beside + 2, 4)


def dispatch(buffer, collective):
    experts, capacity, width = buffer.shape

    def kernel(in_ref, out_ref, sent, arrived, own_sem):
        me, shard = lax.axis_index("expert"), lax.axis_index("shard")
        beside, across, _ = square(shard)
        greet(
            [("expert", lax.rem(me + step, experts)) for step in range(1, experts)]
            + [("shard", beside), ("shard", across)]
        )
        first = []
        for step in range(1, experts):
            peer = lax.rem(me + step, experts)
            copy = remote(
                in_ref.at[peer],
                out_ref.at[shard, me],
                sent.at[0, step],
                arrived.at[0, step],
                "expert",
                peer,
            )
            copy.start()
            first.append(copy)
        own = pltpu.make_async_copy(in_ref.at[me], out_ref.at[shard, me], own_sem)
        own.start()
        near, far, last = [], [], []
        for step in range(experts):
            origin = lax.rem(me + experts - step, experts)
            if step:
                first[step - 1].wait_recv()
            else:
                own.wait()
            block = out_ref.at[shard, origin]
            copy = remote(block, block, sent.at[2, step], arrived.at[2, step], "shard", across)
            copy.start()
            far.append(copy)
            copy = remote(block, block, sent.at[1, step], arrived.at[1, step], "shard", beside)
            copy.start()
            near.append(copy)
        for step in range(experts):
            origin = lax.rem(me + experts - step, experts)
            far[step].wait_recv()
            block = out_ref.at[across, origin]
            copy = remote(block, block, sent.at[3, step], arrived.at[3, step], "shard", beside)
            copy.start()
            last.append(copy)
        for copy in first + far:
            copy.wait_send()
        for copy in near + last:
            copy.wait()

    return call(
        kernel,
        jax.ShapeDtypeStruct((4, experts, capacity, width), buffer.dtype),
        [DMA((4, experts)), DMA((4, experts)), DMA],
        collective,
        (buffer,),
    )


def give_back(parts, collective):
    _, experts, capacity, width = parts.shape
    block_shape = (experts, capacity, width)

    def kernel(in_ref, out_ref, pair, own_sum, send_sum, far_sum, ready, sent, arrived, own_sem):
        me, shard = lax.axis_index("expert"), lax.axis_index("shard")
        beside, across, corner = square(shard)
        greet(
            [("expert", lax.rem(me + step, experts)) for step in range(1, experts)]
            + [("shard", beside), ("shard", across)]
        )
        near, far, last = [], [], []
        for step in range(experts):
            peer = lax.rem(me + step + 1, experts)
            for which, quarter in ((0, corner), (1, beside)):
                copy = remote(
                    in_ref.at[quarter, peer],
                    pair.at[which, step],
                    sent.at[which, step],
                    arrived.at[which, step],
                    "shard",
                    beside,
                )
                copy.start()
                near.append(copy)
        for step in range(experts):
            peer = lax.rem(me + step + 1, experts)
            near[2 * step].wait_recv()
            send_sum[step] = (
                in_ref[across, peer].astype(jnp.float32) + pair[0, step].astype(jnp.float32)
            ).astype(jnp.bfloat16)
            copy = remote(
                send_sum.at[step],
                far_sum.at[step],
                sent.at[2, step],
                arrived.at[2, step],
                "shard",
                across,
            )
            copy.start()
            far.append(copy)
            near[2 * step + 1].wait_recv()
            own_sum[step] = in_ref[shard, peer].astype(jnp.float32) + pair[1, step].astype(
                jnp.float32
            )
        for step in range(experts):
            peer = lax.rem(me + step + 1, experts)
            far[step].wait_recv()
            ready[step] = (own_sum[step] + far_sum[step].astype(jnp.float32)).astype(jnp.bfloat16)
            if step < experts - 1:
                copy = remote(
                    ready.at[step],
                    out_ref.at[shard, me],
                    sent.at[3, step],
                    arrived.at[3, step],
                    "expert",
                    peer,
                )
            else:
                copy = pltpu.make_async_copy(ready.at[step], out_ref.at[shard, me], own_sem)
            copy.start()
            last.append(copy)
        side, over, rest = [], [], []
        for step in range(experts):
            origin = lax.rem(me + 2 * experts - step - 1, experts)
            if step < experts - 1:
                last[step].wait_recv()
            else:
                last[step].wait()
            block = out_ref.at[shard, origin]
            copy = remote(block, block, sent.at[5, step], arrived.at[5, step], "shard", across)
            copy.start()
            over.append(copy)
            copy = remote(block, block, sent.at[4, step], arrived.at[4, step], "shard", beside)
            copy.start()
            side.append(copy)
        for step in range(experts):
            origin = lax.rem(me + 2 * experts - step - 1, experts)
            over[step].wait_recv()
            block = out_ref.at[across, origin]
            copy = remote(block, block, sent.at[6, step], arrived.at[6, step], "shard", beside)
            copy.start()
            rest.append(copy)
        for copy in near + far + last[: experts - 1] + over:
            copy.wait_send()
        for copy in side + rest:
            copy.wait()

    return call(
        kernel,
        jax.ShapeDtypeStruct(parts.shape, jnp.bfloat16),
        [
            pltpu.VMEM((2,) + block_shape, jnp.bfloat16),
            pltpu.VMEM(block_shape, jnp.float32),
            pltpu.VMEM(block_shape, jnp.bfloat16),
            pltpu.VMEM(block_shape, jnp.bfloat16),
            pltpu.VMEM(block_shape, jnp.bfloat16),
            DMA((7, experts)),
            DMA((7, experts)),
            DMA,
        ],
        collective,
        (parts,),
    )


def gather_pairs(operands, collective):
    count = lax.axis_size("expert")
    half = count // 2
    total = len(operands)

    def kernel(*refs):
        ins, outs = refs[:total], refs[total : 2 * total]
        sent, arrived, own_sem = refs[2 * total :]
        me = lax.axis_index("expert")
        mate = me + 1 - 2 * lax.rem(me, 2)
        column = [lax.rem(me + 2 * step, count) for step in range(1, half)]
        greet([("expert", peer) for peer in column + [mate]])
        first, second = [], []
        for step in range(1, half):
            for index in range(total):
                copy = remote(
                    ins[index],
                    outs[index].at[me],
                    sent.at[0, index, step],
                    arrived.at[0, index, step],
                    "expert",
                    column[step - 1],
                )
                copy.start()
                first.append(copy)
        own = []
        for index in range(total):
            copy = remote(
                ins[index],
                outs[index].at[me],
                sent.at[1, index, 0],
                arrived.at[1, index, 0],
                "expert",
                mate,
            )
            copy.start()
            second.append(copy)
            copy = pltpu.make_async_copy(ins[index], outs[index].at[me], own_sem.at[index])
            copy.start()
            own.append(copy)
        for step in range(1, half):
            origin = lax.rem(me + count - 2 * step, count)
            for index in range(total):
                first[(step - 1) * total + index].wait_recv()
                block = outs[index].at[origin]
                copy = remote(
                    block,
                    block,
                    sent.at[1, index, step],
                    arrived.at[1, index, step],
                    "expert",
                    mate,
                )
                copy.start()
                second.append(copy)
        for copy in first:
            copy.wait_send()
        for copy in second + own:
            copy.wait()

    out_shape = [jax.ShapeDtypeStruct((count,) + x.shape, x.dtype) for x in operands]
    scratch = [DMA((2, total, half)), DMA((2, total, half)), DMA((total,))]
    return call(kernel, out_shape, scratch, collective, operands)


def reduce_pairs(spread, collective):
    count = spread.shape[0]
    half = count // 2
    shape = (half,) + spread.shape[1:]
    order = list(range(1, half)) + [0]

    def kernel(in_ref, out_ref, pair, ready, sent, arrived):
        me = lax.axis_index("expert")
        mate = me + 1 - 2 * lax.rem(me, 2)
        column = [lax.rem(me + 2 * step, count) for step in range(half)]
        greet([("expert", peer) for peer in column[1:] + [mate]])
        first, second = [], []
        for step in order:
            copy = remote(
                in_ref.at[lax.rem(mate + 2 * step, count)],
                pair.at[step],
                sent.at[0, step],
                arrived.at[0, step],
                "expert",
                mate,
            )
            copy.start()
            first.append(copy)
        for position, step in enumerate(order):
            first[position].wait_recv()
            value = (
                in_ref[column[step]].astype(jnp.float32) + pair[step].astype(jnp.float32)
            ).astype(jnp.bfloat16)
            if step == 0:
                out_ref[0] = value
            else:
                ready[step] = value
                copy = remote(
                    ready.at[step],
                    out_ref.at[step],
                    sent.at[1, step],
                    arrived.at[1, step],
                    "expert",
                    column[step],
                )
                copy.start()
                second.append(copy)
        for copy in first:
            copy.wait_send()
        for copy in second:
            copy.wait()

    return call(
        kernel,
        jax.ShapeDtypeStruct(shape, spread.dtype),
        [
            pltpu.VMEM(shape, spread.dtype),
            pltpu.VMEM(shape, spread.dtype),
            DMA((2, half)),
            DMA((2, half)),
        ],
        collective,
        (spread,),
    )


def sum_shards(part, collective):
    (gathered,) = exchange("shard", collective, (), (part.astype(jnp.bfloat16),))
    return jnp.sum(gathered.astype(jnp.float32), axis=0)


def local(
    block_in,
    qkv_weight,
    out_weight,
    norm1_gain,
    norm2_gain,
    router_weight,
    rel_bias,
    expert_in,
    expert_out,
    routes,
    cotangent,
):
    length, model_width = block_in.shape
    experts = lax.axis_size("expert")
    capacity = 4 * length // experts
    score_scale = 1.0 / math.sqrt(HEAD_DIM)
    shards = lax.axis_size("shard")
    shard = lax.axis_index("shard")
    rows = capacity // shards
    small = jnp.concatenate([norm1_gain[None], norm2_gain[None], router_weight.T], axis=0)
    weights = jnp.concatenate([qkv_weight, out_weight[None]], axis=0)
    weights_all, small_all = gather_pairs((weights, small), 0)
    weights_all = weights_all.transpose(1, 0, 2, 3).reshape(4, model_width, -1)
    small_all = small_all.transpose(1, 0, 2).reshape(-1, model_width)
    qkv_full, out_full = weights_all[:3], weights_all[3]
    gain_low_one, gain_low_two, router = small_all[0], small_all[1], small_all[2:].T
    gain_one = gain_low_one.astype(jnp.float32)
    gain_two = gain_low_two.astype(jnp.float32)
    inputs = block_in.astype(jnp.float32)
    normed_one, inverse_one = normalize(inputs)
    hidden_one = (normed_one * gain_one).astype(jnp.bfloat16)
    projected = jnp.einsum(
        "td,cdj->ctj", hidden_one, qkv_full, preferred_element_type=jnp.float32
    ).astype(jnp.bfloat16)
    local_width = projected.shape[2]
    local_heads = local_width // HEAD_DIM
    queries = projected[0].reshape(length, local_heads, HEAD_DIM)
    keys_local = projected[1].reshape(length, local_heads, HEAD_DIM)
    values_local = projected[2].reshape(length, local_heads, HEAD_DIM)
    onehot_bucket = bucket_onehot(length)
    per_distance = jnp.dot(onehot_bucket, rel_bias, precision=lax.Precision.HIGHEST).T
    bias_full = toeplitz(per_distance)
    causal = lax.broadcasted_iota(jnp.int32, (length, length), 0) >= lax.broadcasted_iota(
        jnp.int32, (length, length), 1
    )

    def scores_of():
        raw_scores = (
            jnp.einsum("ihd,jhd->hij", queries, keys_local, preferred_element_type=jnp.float32)
            * score_scale
            + bias_full
        )
        return jnp.where(causal[None], raw_scores, -jnp.inf)

    scores = scores_of()
    log_total = jnp.log(jnp.sum(jnp.exp(scores), axis=-1))
    attention_low = jnp.exp(scores - log_total[..., None]).astype(jnp.bfloat16)
    attended = (
        jnp.einsum("hij,jhd->ihd", attention_low, values_local, preferred_element_type=jnp.float32)
        .astype(jnp.bfloat16)
        .reshape(length, local_width)
    )
    attn_part = jnp.einsum("tc,mc->tm", attended, out_full, preferred_element_type=jnp.float32)
    residual_one = inputs + sum_shards(attn_part, 1)
    normed_two, inverse_two = normalize(residual_one)
    hidden_two = (normed_two * gain_two).astype(jnp.bfloat16)
    logits = jnp.dot(hidden_two, router, preferred_element_type=jnp.float32)
    expert_ids = lax.broadcasted_iota(jnp.int32, (1, 1, router.shape[1]), 2)
    route_hot = (routes[:, :, None] == expert_ids).astype(jnp.float32)
    chosen = jnp.sum(logits[:, None, :] * route_hot, axis=-1)
    chosen_exp = jnp.exp(chosen)
    gate_value = chosen_exp / jnp.sum(chosen_exp, axis=1, keepdims=True)
    flat_routes = routes.reshape(-1)
    counts_hot = (flat_routes[:, None] == expert_ids[0]).astype(jnp.int32)
    slot_index = jnp.sum((jnp.cumsum(counts_hot, axis=0) - 1) * counts_hot, axis=1)
    slot_target = flat_routes * capacity + slot_index
    upstream = cotangent.astype(jnp.float32)

    slots = experts * capacity
    target_pair = slot_target.reshape(length, 2)
    position = lax.broadcasted_iota(jnp.int32, (slots, length), 0)
    slot_id = (
        (position // rows) % experts * capacity
        + position // (rows * experts) * rows
        + position % rows
    )
    place = [(slot_id == target_pair[:, k][None, :]).astype(jnp.bfloat16) for k in range(2)]
    mine = [lax.dynamic_slice_in_dim(p, shard * rows * experts, rows * experts) for p in place]
    slot_grad = [(gate_value[:, k : k + 1] * upstream).astype(jnp.bfloat16) for k in range(2)]
    outgoing = jnp.concatenate(
        [
            jnp.dot(mine[0] + mine[1], hidden_two, preferred_element_type=jnp.float32),
            jnp.dot(mine[0], slot_grad[0], preferred_element_type=jnp.float32)
            + jnp.dot(mine[1], slot_grad[1], preferred_element_type=jnp.float32),
        ],
        axis=1,
    ).astype(jnp.bfloat16)
    incoming = dispatch(outgoing.reshape(experts, rows, 2 * model_width), 2).reshape(
        slots, 2 * model_width
    )
    arrived, arrived_grad = incoming[:, :model_width], incoming[:, model_width:]
    pre_act = jnp.dot(arrived, expert_in[0], preferred_element_type=jnp.float32)
    activated, gelu_slope = gelu_parts(pre_act)
    act_low = activated.astype(jnp.bfloat16)
    expert_part = jnp.dot(act_low, expert_out[0], preferred_element_type=jnp.float32)
    act_grad = jnp.einsum(
        "rd,fd->rf", arrived_grad, expert_out[0], preferred_element_type=jnp.float32
    )
    pre_grad = (act_grad * gelu_slope).astype(jnp.bfloat16)
    row_part = jnp.einsum("rf,df->rd", pre_grad, expert_in[0], preferred_element_type=jnp.float32)
    parts = jnp.concatenate(
        [expert_part.astype(jnp.bfloat16), row_part.astype(jnp.bfloat16)], axis=1
    ).reshape(shards, experts, rows, 2 * model_width)
    returned = give_back(parts, 3).reshape(slots, 2 * model_width)
    pair_rows = [
        jnp.einsum("sp,sc->pc", p, returned, preferred_element_type=jnp.float32) for p in place
    ]
    values = [r[:, :model_width] for r in pair_rows]
    block_out = (
        residual_one + gate_value[:, 0:1] * values[0] + gate_value[:, 1:2] * values[1]
    ).astype(jnp.bfloat16)
    gate_grad = jnp.stack([jnp.sum(upstream * v, axis=-1) for v in values], axis=1)
    logit_pair = gate_value * (gate_grad - jnp.sum(gate_value * gate_grad, axis=1, keepdims=True))
    logit_grad = jnp.sum(logit_pair[:, :, None] * route_hot, axis=1).astype(jnp.bfloat16)
    router_local = jnp.einsum(
        "td,te->ed", hidden_two, logit_grad, preferred_element_type=jnp.float32
    )
    from_router = jnp.einsum("te,de->td", logit_grad, router, preferred_element_type=jnp.float32)
    expert_out_local = jnp.einsum(
        "rf,rd->fd", act_low, arrived_grad, preferred_element_type=jnp.float32
    )
    expert_in_local = jnp.einsum("rd,rf->df", arrived, pre_grad, preferred_element_type=jnp.float32)
    hidden_two_grad = pair_rows[0][:, model_width:] + pair_rows[1][:, model_width:] + from_router
    gain_two_grad = jnp.sum(hidden_two_grad * normed_two, axis=0)
    residual_grad = upstream + norm_back(hidden_two_grad, normed_two, inverse_two, gain_two)
    residual_low = residual_grad.astype(jnp.bfloat16)
    out_local = jnp.einsum("tm,tc->mc", residual_low, attended, preferred_element_type=jnp.float32)
    attended_grad = (
        jnp.einsum("tm,mc->tc", residual_low, out_full, preferred_element_type=jnp.float32)
        .astype(jnp.bfloat16)
        .reshape(length, local_heads, HEAD_DIM)
    )
    scores = scores_of()
    attention = jnp.exp(scores - log_total[..., None])
    attention_low = attention.astype(jnp.bfloat16)
    value_grad = jnp.einsum(
        "hij,ihd->jhd", attention_low, attended_grad, preferred_element_type=jnp.float32
    )
    prob_grad = jnp.einsum(
        "ihd,jhd->hij", attended_grad, values_local, preferred_element_type=jnp.float32
    )
    row_delta = jnp.sum(
        attended_grad.astype(jnp.float32)
        * attended.reshape(length, local_heads, HEAD_DIM).astype(jnp.float32),
        axis=-1,
    ).T
    score_grad = attention * (prob_grad - row_delta[:, :, None])
    bias_local = jnp.dot(
        onehot_bucket.T, diagonal_sums(score_grad).T, precision=lax.Precision.HIGHEST
    )
    score_low = score_grad.astype(jnp.bfloat16)
    query_grad = (
        jnp.einsum("hij,jhd->ihd", score_low, keys_local, preferred_element_type=jnp.float32)
        * score_scale
    ).astype(jnp.bfloat16)
    key_grad = (
        jnp.einsum("hij,ihd->jhd", score_low, queries, preferred_element_type=jnp.float32)
        * score_scale
    ).astype(jnp.bfloat16)
    stacked = jnp.stack([query_grad, key_grad, value_grad.astype(jnp.bfloat16)]).reshape(
        3, length, local_width
    )
    qkv_local = jnp.einsum("td,ctj->cdj", hidden_one, stacked, preferred_element_type=jnp.float32)
    hidden_one_part = jnp.einsum(
        "ctj,cdj->td", stacked, qkv_full, preferred_element_type=jnp.float32
    )
    hidden_one_grad = sum_shards(hidden_one_part, 5)
    gain_one_grad = jnp.sum(hidden_one_grad * normed_one, axis=0)
    input_grad = residual_grad + norm_back(hidden_one_grad, normed_one, inverse_one, gain_one)
    grads = jnp.concatenate([qkv_local, out_local[None]], axis=0).astype(jnp.bfloat16)
    grads = grads.reshape(4, experts, -1, local_width).transpose(1, 0, 2, 3)
    small_grads = jnp.concatenate([gain_one_grad[None], gain_two_grad[None], router_local], axis=0)
    small_grads = small_grads.reshape(small_grads.shape[0], experts, -1).transpose(1, 0, 2)
    grads_all = reduce_pairs(grads, 6)
    small_grads_all, bias_all = exchange("expert", 4, (small_grads,), (bias_local.T,))
    grads_sum = jnp.sum(grads_all.astype(jnp.float32), axis=0)
    small_sum = jnp.sum(small_grads_all, axis=0)
    qkv_grad, out_grad = grads_sum[:3], grads_sum[3]
    norm1_grad, norm2_grad, router_grad = small_sum[0], small_sum[1], small_sum[2:].T
    bias_grad = jnp.sum(bias_all, axis=0).T
    return (
        block_out,
        input_grad,
        qkv_grad,
        out_grad,
        norm1_grad,
        norm2_grad,
        router_grad,
        bias_grad,
        expert_in_local[None],
        expert_out_local[None],
    )


def solution(mesh):
    placed = (
        P("expert", None),
        P(None, "expert", "shard"),
        P("expert", "shard"),
        P("expert"),
        P("expert"),
        P("expert", None),
        P(None, "shard"),
        P("expert", None, "shard"),
        P("expert", "shard", None),
        P("expert", None),
        P("expert", None),
    )
    return jax.shard_map(
        local,
        mesh=mesh,
        in_specs=placed,
        out_specs=(
            P("expert", None),
            P("expert", None),
            P(None, "expert", "shard"),
            P("expert", "shard"),
            P("expert"),
            P("expert"),
            P("expert", None),
            P(None, "shard"),
            P("expert", None, "shard"),
            P("expert", "shard", None),
        ),
        check_vma=False,
    )
```

```python
import math

import jax
import jax.numpy as jnp
from jax import lax
from jax.experimental import pallas as pl
from jax.experimental.pallas import tpu as pltpu
from jax.sharding import PartitionSpec as P

HEAD_DIM = 64
BUCKETS = 32
MAX_DIST = 128


EPS = 1e-06


def bucket_edges():
    exact_count = BUCKETS // 2
    edge_list = []
    for bucket_id in range(1, BUCKETS):
        if bucket_id < exact_count:
            edge_list.append(bucket_id)
        else:
            edge_list.append(
                math.ceil(
                    exact_count
                    * (MAX_DIST / exact_count)
                    ** ((bucket_id - exact_count) / (BUCKETS - exact_count))
                )
            )
    return jnp.array(edge_list, dtype=jnp.int32)


def bucket_onehot(length):
    distance = lax.broadcasted_iota(jnp.int32, (length, 1), 0)
    bucket = jnp.sum((distance >= bucket_edges()[None, :]).astype(jnp.int32), axis=1)
    return (bucket[:, None] == lax.broadcasted_iota(jnp.int32, (length, BUCKETS), 1)).astype(
        jnp.float32
    )


def toeplitz(per_distance):
    head_count, length = per_distance.shape
    widened = jnp.concatenate(
        [jnp.zeros((head_count, length - 1), per_distance.dtype), per_distance], axis=1
    )
    rows_flat = jnp.broadcast_to(widened[:, None, :], (head_count, length, 2 * length - 1)).reshape(
        head_count, -1
    )
    shifted = jnp.pad(rows_flat, ((0, 0), (0, length))).reshape(head_count, length, 2 * length)[
        :, :, :length
    ]
    return jnp.flip(shifted, axis=2)


def diagonal_sums(matrix):
    head_count, length, _ = matrix.shape
    padded = jnp.pad(jnp.flip(matrix, axis=2), ((0, 0), (0, 0), (0, length))).reshape(
        head_count, -1
    )
    skewed = padded[:, : length * (2 * length - 1)].reshape(head_count, length, 2 * length - 1)
    return jnp.sum(skewed, axis=1)[:, length - 1 :]


def gelu_parts(pre_act):
    cumulative = 0.5 * (1.0 + jax.scipy.special.erf(pre_act * (1.0 / math.sqrt(2.0))))
    density = jnp.exp(-0.5 * pre_act * pre_act) * (1.0 / math.sqrt(2.0 * math.pi))
    return (pre_act * cumulative, cumulative + pre_act * density)


def normalize(matrix):
    inverse = lax.rsqrt(jnp.mean(matrix * matrix, axis=-1, keepdims=True) + EPS)
    return (matrix * inverse, inverse)


def norm_back(upstream, normed, inverse, gain_vector):
    scaled = upstream * gain_vector
    return inverse * (scaled - normed * jnp.mean(scaled * normed, axis=-1, keepdims=True))


MESH = pl.DeviceIdType.MESH
DMA = pltpu.SemaphoreType.DMA


def remote(source, target, sent, arrived, axis, peer):
    return pltpu.make_async_remote_copy(
        src_ref=source,
        dst_ref=target,
        send_sem=sent,
        recv_sem=arrived,
        device_id={axis: peer},
        device_id_type=MESH,
    )


def greet(axis_peers):
    barrier = pltpu.get_barrier_semaphore()
    for axis, peer in axis_peers:
        pl.semaphore_signal(barrier, inc=1, device_id={axis: peer}, device_id_type=MESH)
    pl.semaphore_wait(barrier, len(axis_peers))


def call(kernel, out_shape, scratch, collective, operands):
    vmem = pl.BlockSpec(memory_space=pltpu.VMEM)
    return pl.pallas_call(
        kernel,
        out_shape=out_shape,
        in_specs=[vmem] * len(operands),
        out_specs=jax.tree.map(lambda _: vmem, out_shape),
        scratch_shapes=scratch,
        compiler_params=pltpu.CompilerParams(collective_id=collective, has_side_effects=True),
    )(*operands)


def exchange(axis, collective, spread, shared):
    count = lax.axis_size(axis)
    operands = tuple(spread) + tuple(shared)
    total = len(operands)

    def kernel(*refs):
        ins, outs = refs[:total], refs[total : 2 * total]
        sent, arrived, own_sem = refs[2 * total :]
        me = lax.axis_index(axis)
        greet([(axis, lax.rem(me + step, count)) for step in range(1, count)])
        copies = []
        for step in range(1, count):
            peer = lax.rem(me + step, count)
            for index in range(total):
                source = ins[index].at[peer] if index < len(spread) else ins[index]
                copy = remote(
                    source,
                    outs[index].at[me],
                    sent.at[index, step],
                    arrived.at[index, step],
                    axis,
                    peer,
                )
                copy.start()
                copies.append(copy)
        for index in range(total):
            source = ins[index].at[me] if index < len(spread) else ins[index]
            copy = pltpu.make_async_copy(source, outs[index].at[me], own_sem.at[index])
            copy.start()
            copies.append(copy)
        for copy in copies:
            copy.wait()

    out_shape = [jax.ShapeDtypeStruct(x.shape, x.dtype) for x in spread] + [
        jax.ShapeDtypeStruct((count,) + x.shape, x.dtype) for x in shared
    ]
    scratch = [DMA((total, count)), DMA((total, count)), DMA((total,))]
    return call(kernel, out_shape, scratch, collective, operands)


def square(shard):
    beside = shard + 1 - 2 * lax.rem(shard, 2)
    across = lax.rem(shard + 2, 4)
    return beside, across, lax.rem(beside + 2, 4)


def dispatch(buffer, collective):
    experts, capacity, width = buffer.shape

    def kernel(in_ref, out_ref, sent, arrived, own_sem):
        me, shard = lax.axis_index("expert"), lax.axis_index("shard")
        beside, across, _ = square(shard)
        greet(
            [("expert", lax.rem(me + step, experts)) for step in range(1, experts)]
            + [("shard", beside), ("shard", across)]
        )
        first = []
        for step in range(1, experts):
            peer = lax.rem(me + step, experts)
            copy = remote(
                in_ref.at[peer],
                out_ref.at[shard, me],
                sent.at[0, step],
                arrived.at[0, step],
                "expert",
                peer,
            )
            copy.start()
            first.append(copy)
        own = pltpu.make_async_copy(in_ref.at[me], out_ref.at[shard, me], own_sem)
        own.start()
        near, far, last = [], [], []
        for step in range(experts):
            origin = lax.rem(me + experts - step, experts)
            if step:
                first[step - 1].wait_recv()
            else:
                own.wait()
            block = out_ref.at[shard, origin]
            copy = remote(block, block, sent.at[2, step], arrived.at[2, step], "shard", across)
            copy.start()
            far.append(copy)
            copy = remote(block, block, sent.at[1, step], arrived.at[1, step], "shard", beside)
            copy.start()
            near.append(copy)
        for step in range(experts):
            origin = lax.rem(me + experts - step, experts)
            far[step].wait_recv()
            block = out_ref.at[across, origin]
            copy = remote(block, block, sent.at[3, step], arrived.at[3, step], "shard", beside)
            copy.start()
            last.append(copy)
        for copy in first + far:
            copy.wait_send()
        for copy in near + last:
            copy.wait()

    return call(
        kernel,
        jax.ShapeDtypeStruct((4, experts, capacity, width), buffer.dtype),
        [DMA((4, experts)), DMA((4, experts)), DMA],
        collective,
        (buffer,),
    )


def give_back(parts, collective):
    _, experts, capacity, width = parts.shape
    block_shape = (experts, capacity, width)

    def kernel(in_ref, out_ref, pair, own_sum, send_sum, far_sum, ready, sent, arrived, own_sem):
        me, shard = lax.axis_index("expert"), lax.axis_index("shard")
        beside, across, corner = square(shard)
        greet(
            [("expert", lax.rem(me + step, experts)) for step in range(1, experts)]
            + [("shard", beside), ("shard", across)]
        )
        near, far, last = [], [], []
        for step in range(experts):
            peer = lax.rem(me + step + 1, experts)
            for which, quarter in ((0, corner), (1, beside)):
                copy = remote(
                    in_ref.at[quarter, peer],
                    pair.at[which, step],
                    sent.at[which, step],
                    arrived.at[which, step],
                    "shard",
                    beside,
                )
                copy.start()
                near.append(copy)
        for step in range(experts):
            peer = lax.rem(me + step + 1, experts)
            near[2 * step].wait_recv()
            send_sum[step] = (
                in_ref[across, peer].astype(jnp.float32) + pair[0, step].astype(jnp.float32)
            ).astype(jnp.bfloat16)
            copy = remote(
                send_sum.at[step],
                far_sum.at[step],
                sent.at[2, step],
                arrived.at[2, step],
                "shard",
                across,
            )
            copy.start()
            far.append(copy)
            near[2 * step + 1].wait_recv()
            own_sum[step] = in_ref[shard, peer].astype(jnp.float32) + pair[1, step].astype(
                jnp.float32
            )
        for step in range(experts):
            peer = lax.rem(me + step + 1, experts)
            far[step].wait_recv()
            ready[step] = (own_sum[step] + far_sum[step].astype(jnp.float32)).astype(jnp.bfloat16)
            if step < experts - 1:
                copy = remote(
                    ready.at[step],
                    out_ref.at[shard, me],
                    sent.at[3, step],
                    arrived.at[3, step],
                    "expert",
                    peer,
                )
            else:
                copy = pltpu.make_async_copy(ready.at[step], out_ref.at[shard, me], own_sem)
            copy.start()
            last.append(copy)
        side, over, rest = [], [], []
        for step in range(experts):
            origin = lax.rem(me + 2 * experts - step - 1, experts)
            if step < experts - 1:
                last[step].wait_recv()
            else:
                last[step].wait()
            block = out_ref.at[shard, origin]
            copy = remote(block, block, sent.at[5, step], arrived.at[5, step], "shard", across)
            copy.start()
            over.append(copy)
            copy = remote(block, block, sent.at[4, step], arrived.at[4, step], "shard", beside)
            copy.start()
            side.append(copy)
        for step in range(experts):
            origin = lax.rem(me + 2 * experts - step - 1, experts)
            over[step].wait_recv()
            block = out_ref.at[across, origin]
            copy = remote(block, block, sent.at[6, step], arrived.at[6, step], "shard", beside)
            copy.start()
            rest.append(copy)
        for copy in near + far + last[: experts - 1] + over:
            copy.wait_send()
        for copy in side + rest:
            copy.wait()

    return call(
        kernel,
        jax.ShapeDtypeStruct(parts.shape, jnp.bfloat16),
        [
            pltpu.VMEM((2,) + block_shape, jnp.bfloat16),
            pltpu.VMEM(block_shape, jnp.float32),
            pltpu.VMEM(block_shape, jnp.bfloat16),
            pltpu.VMEM(block_shape, jnp.bfloat16),
            pltpu.VMEM(block_shape, jnp.bfloat16),
            DMA((7, experts)),
            DMA((7, experts)),
            DMA,
        ],
        collective,
        (parts,),
    )


def gather_pairs(operands, collective):
    count = lax.axis_size("expert")
    half = count // 2
    total = len(operands)

    def kernel(*refs):
        ins, outs = refs[:total], refs[total : 2 * total]
        sent, arrived, own_sem = refs[2 * total :]
        me = lax.axis_index("expert")
        mate = me + 1 - 2 * lax.rem(me, 2)
        column = [lax.rem(me + 2 * step, count) for step in range(1, half)]
        greet([("expert", peer) for peer in column + [mate]])
        first, second = [], []
        for step in range(1, half):
            for index in range(total):
                copy = remote(
                    ins[index],
                    outs[index].at[me],
                    sent.at[0, index, step],
                    arrived.at[0, index, step],
                    "expert",
                    column[step - 1],
                )
                copy.start()
                first.append(copy)
        own = []
        for index in range(total):
            copy = remote(
                ins[index],
                outs[index].at[me],
                sent.at[1, index, 0],
                arrived.at[1, index, 0],
                "expert",
                mate,
            )
            copy.start()
            second.append(copy)
            copy = pltpu.make_async_copy(ins[index], outs[index].at[me], own_sem.at[index])
            copy.start()
            own.append(copy)
        for step in range(1, half):
            origin = lax.rem(me + count - 2 * step, count)
            for index in range(total):
                first[(step - 1) * total + index].wait_recv()
                block = outs[index].at[origin]
                copy = remote(
                    block,
                    block,
                    sent.at[1, index, step],
                    arrived.at[1, index, step],
                    "expert",
                    mate,
                )
                copy.start()
                second.append(copy)
        for copy in first:
            copy.wait_send()
        for copy in second + own:
            copy.wait()

    out_shape = [jax.ShapeDtypeStruct((count,) + x.shape, x.dtype) for x in operands]
    scratch = [DMA((2, total, half)), DMA((2, total, half)), DMA((total,))]
    return call(kernel, out_shape, scratch, collective, operands)


def reduce_pairs(spread, collective):
    count = spread.shape[0]
    half = count // 2
    shape = (half,) + spread.shape[1:]
    order = list(range(1, half)) + [0]

    def kernel(in_ref, out_ref, pair, ready, sent, arrived):
        me = lax.axis_index("expert")
        mate = me + 1 - 2 * lax.rem(me, 2)
        column = [lax.rem(me + 2 * step, count) for step in range(half)]
        greet([("expert", peer) for peer in column[1:] + [mate]])
        first, second = [], []
        for step in order:
            copy = remote(
                in_ref.at[lax.rem(mate + 2 * step, count)],
                pair.at[step],
                sent.at[0, step],
                arrived.at[0, step],
                "expert",
                mate,
            )
            copy.start()
            first.append(copy)
        for position, step in enumerate(order):
            first[position].wait_recv()
            value = (
                in_ref[column[step]].astype(jnp.float32) + pair[step].astype(jnp.float32)
            ).astype(jnp.bfloat16)
            if step == 0:
                out_ref[0] = value
            else:
                ready[step] = value
                copy = remote(
                    ready.at[step],
                    out_ref.at[step],
                    sent.at[1, step],
                    arrived.at[1, step],
                    "expert",
                    column[step],
                )
                copy.start()
                second.append(copy)
        for copy in first:
            copy.wait_send()
        for copy in second:
            copy.wait()

    return call(
        kernel,
        jax.ShapeDtypeStruct(shape, spread.dtype),
        [
            pltpu.VMEM(shape, spread.dtype),
            pltpu.VMEM(shape, spread.dtype),
            DMA((2, half)),
            DMA((2, half)),
        ],
        collective,
        (spread,),
    )


def sum_shards(part, collective):
    (gathered,) = exchange("shard", collective, (), (part.astype(jnp.bfloat16),))
    return jnp.sum(gathered.astype(jnp.float32), axis=0)


def local(
    block_in,
    qkv_weight,
    out_weight,
    norm1_gain,
    norm2_gain,
    router_weight,
    rel_bias,
    expert_in,
    expert_out,
    routes,
    cotangent,
):
    length, model_width = block_in.shape
    experts = lax.axis_size("expert")
    capacity = 4 * length // experts
    score_scale = 1.0 / math.sqrt(HEAD_DIM)
    shards = lax.axis_size("shard")
    shard = lax.axis_index("shard")
    rows = capacity // shards
    small = jnp.concatenate([norm1_gain[None], norm2_gain[None], router_weight.T], axis=0)
    weights = jnp.concatenate([qkv_weight[0], qkv_weight[1], qkv_weight[2], out_weight], axis=1)
    weights_all, small_all = gather_pairs((weights, small), 0)
    weights_all = weights_all.reshape(model_width, -1)
    small_all = small_all.transpose(1, 0, 2).reshape(-1, model_width)
    local_width = out_weight.shape[1]
    qkv_full, out_full = weights_all[:, : 3 * local_width], weights_all[:, 3 * local_width :]
    gain_low_one, gain_low_two, router = small_all[0], small_all[1], small_all[2:].T
    gain_one = gain_low_one.astype(jnp.float32)
    gain_two = gain_low_two.astype(jnp.float32)
    inputs = block_in.astype(jnp.float32)
    normed_one, inverse_one = normalize(inputs)
    hidden_one = (normed_one * gain_one).astype(jnp.bfloat16)
    projected_flat = jnp.dot(
        hidden_one, qkv_full, preferred_element_type=jnp.float32
    ).astype(jnp.bfloat16)
    projected = [projected_flat[:, c * local_width : (c + 1) * local_width] for c in range(3)]
    local_heads = local_width // HEAD_DIM
    queries = projected[0].reshape(length, local_heads, HEAD_DIM)
    keys_local = projected[1].reshape(length, local_heads, HEAD_DIM)
    values_local = projected[2].reshape(length, local_heads, HEAD_DIM)
    onehot_bucket = bucket_onehot(length)
    per_distance = jnp.dot(onehot_bucket, rel_bias, precision=lax.Precision.HIGHEST).T
    bias_full = toeplitz(per_distance)
    causal = lax.broadcasted_iota(jnp.int32, (length, length), 0) >= lax.broadcasted_iota(
        jnp.int32, (length, length), 1
    )

    def scores_of():
        raw_scores = (
            jnp.einsum("ihd,jhd->hij", queries, keys_local, preferred_element_type=jnp.float32)
            * score_scale
            + bias_full
        )
        return jnp.where(causal[None], raw_scores, -jnp.inf)

    scores = scores_of()
    log_total = jnp.log(jnp.sum(jnp.exp(scores), axis=-1))
    attention_low = jnp.exp(scores - log_total[..., None]).astype(jnp.bfloat16)
    attended = (
        jnp.einsum("hij,jhd->ihd", attention_low, values_local, preferred_element_type=jnp.float32)
        .astype(jnp.bfloat16)
        .reshape(length, local_width)
    )
    attn_part = jnp.einsum("tc,mc->tm", attended, out_full, preferred_element_type=jnp.float32)
    residual_one = inputs + sum_shards(attn_part, 1)
    normed_two, inverse_two = normalize(residual_one)
    hidden_two = (normed_two * gain_two).astype(jnp.bfloat16)
    logits = jnp.dot(hidden_two, router, preferred_element_type=jnp.float32)
    expert_ids = lax.broadcasted_iota(jnp.int32, (1, 1, router.shape[1]), 2)
    route_hot = (routes[:, :, None] == expert_ids).astype(jnp.float32)
    chosen = jnp.sum(logits[:, None, :] * route_hot, axis=-1)
    chosen_exp = jnp.exp(chosen)
    gate_value = chosen_exp / jnp.sum(chosen_exp, axis=1, keepdims=True)
    flat_routes = routes.reshape(-1)
    counts_hot = (flat_routes[:, None] == expert_ids[0]).astype(jnp.int32)
    slot_index = jnp.sum((jnp.cumsum(counts_hot, axis=0) - 1) * counts_hot, axis=1)
    slot_target = flat_routes * capacity + slot_index
    upstream = cotangent.astype(jnp.float32)

    slots = experts * capacity
    target_pair = slot_target.reshape(length, 2)
    position = lax.broadcasted_iota(jnp.int32, (slots, length), 0)
    slot_id = (
        (position // rows) % experts * capacity
        + position // (rows * experts) * rows
        + position % rows
    )
    place = [(slot_id == target_pair[:, k][None, :]).astype(jnp.bfloat16) for k in range(2)]
    mine = [lax.dynamic_slice_in_dim(p, shard * rows * experts, rows * experts) for p in place]
    slot_grad = [(gate_value[:, k : k + 1] * upstream).astype(jnp.bfloat16) for k in range(2)]
    outgoing = jnp.concatenate(
        [
            jnp.dot(mine[0] + mine[1], hidden_two, preferred_element_type=jnp.float32),
            jnp.dot(mine[0], slot_grad[0], preferred_element_type=jnp.float32)
            + jnp.dot(mine[1], slot_grad[1], preferred_element_type=jnp.float32),
        ],
        axis=1,
    ).astype(jnp.bfloat16)
    incoming = dispatch(outgoing.reshape(experts, rows, 2 * model_width), 2).reshape(
        slots, 2 * model_width
    )
    arrived, arrived_grad = incoming[:, :model_width], incoming[:, model_width:]
    pre_act = jnp.dot(arrived, expert_in[0], preferred_element_type=jnp.float32)
    activated, gelu_slope = gelu_parts(pre_act)
    act_low = activated.astype(jnp.bfloat16)
    expert_part = jnp.dot(act_low, expert_out[0], preferred_element_type=jnp.float32)
    act_grad = jnp.einsum(
        "rd,fd->rf", arrived_grad, expert_out[0], preferred_element_type=jnp.float32
    )
    pre_grad = (act_grad * gelu_slope).astype(jnp.bfloat16)
    row_part = jnp.einsum("rf,df->rd", pre_grad, expert_in[0], preferred_element_type=jnp.float32)
    parts = jnp.concatenate(
        [expert_part.astype(jnp.bfloat16), row_part.astype(jnp.bfloat16)], axis=1
    ).reshape(shards, experts, rows, 2 * model_width)
    returned = give_back(parts, 3).reshape(slots, 2 * model_width)
    pair_rows = [
        jnp.einsum("sp,sc->pc", p, returned, preferred_element_type=jnp.float32) for p in place
    ]
    values = [r[:, :model_width] for r in pair_rows]
    block_out = (
        residual_one + gate_value[:, 0:1] * values[0] + gate_value[:, 1:2] * values[1]
    ).astype(jnp.bfloat16)
    gate_grad = jnp.stack([jnp.sum(upstream * v, axis=-1) for v in values], axis=1)
    logit_pair = gate_value * (gate_grad - jnp.sum(gate_value * gate_grad, axis=1, keepdims=True))
    logit_grad = jnp.sum(logit_pair[:, :, None] * route_hot, axis=1).astype(jnp.bfloat16)
    router_local = jnp.einsum(
        "td,te->ed", hidden_two, logit_grad, preferred_element_type=jnp.float32
    )
    from_router = jnp.einsum("te,de->td", logit_grad, router, preferred_element_type=jnp.float32)
    expert_out_local = jnp.einsum(
        "rf,rd->fd", act_low, arrived_grad, preferred_element_type=jnp.float32
    )
    expert_in_local = jnp.einsum("rd,rf->df", arrived, pre_grad, preferred_element_type=jnp.float32)
    hidden_two_grad = pair_rows[0][:, model_width:] + pair_rows[1][:, model_width:] + from_router
    gain_two_grad = jnp.sum(hidden_two_grad * normed_two, axis=0)
    residual_grad = upstream + norm_back(hidden_two_grad, normed_two, inverse_two, gain_two)
    residual_low = residual_grad.astype(jnp.bfloat16)
    out_local = jnp.einsum("tm,tc->mc", residual_low, attended, preferred_element_type=jnp.float32)
    attended_grad = (
        jnp.einsum("tm,mc->tc", residual_low, out_full, preferred_element_type=jnp.float32)
        .astype(jnp.bfloat16)
        .reshape(length, local_heads, HEAD_DIM)
    )
    scores = scores_of()
    attention = jnp.exp(scores - log_total[..., None])
    attention_low = attention.astype(jnp.bfloat16)
    value_grad = jnp.einsum(
        "hij,ihd->jhd", attention_low, attended_grad, preferred_element_type=jnp.float32
    )
    prob_grad = jnp.einsum(
        "ihd,jhd->hij", attended_grad, values_local, preferred_element_type=jnp.float32
    )
    row_delta = jnp.sum(
        attended_grad.astype(jnp.float32)
        * attended.reshape(length, local_heads, HEAD_DIM).astype(jnp.float32),
        axis=-1,
    ).T
    score_grad = attention * (prob_grad - row_delta[:, :, None])
    bias_local = jnp.dot(
        onehot_bucket.T, diagonal_sums(score_grad).T, precision=lax.Precision.HIGHEST
    )
    score_low = score_grad.astype(jnp.bfloat16)
    query_grad = (
        jnp.einsum("hij,jhd->ihd", score_low, keys_local, preferred_element_type=jnp.float32)
        * score_scale
    ).astype(jnp.bfloat16)
    key_grad = (
        jnp.einsum("hij,ihd->jhd", score_low, queries, preferred_element_type=jnp.float32)
        * score_scale
    ).astype(jnp.bfloat16)
    stacked = jnp.concatenate(
        [
            x.reshape(length, local_width)
            for x in (query_grad, key_grad, value_grad.astype(jnp.bfloat16))
        ],
        axis=1,
    )
    qkv_local = jnp.einsum("td,tj->dj", hidden_one, stacked, preferred_element_type=jnp.float32)
    hidden_one_part = jnp.einsum("tj,dj->td", stacked, qkv_full, preferred_element_type=jnp.float32)
    hidden_one_grad = sum_shards(hidden_one_part, 5)
    gain_one_grad = jnp.sum(hidden_one_grad * normed_one, axis=0)
    input_grad = residual_grad + norm_back(hidden_one_grad, normed_one, inverse_one, gain_one)
    grads = jnp.concatenate(
        [qkv_local.astype(jnp.bfloat16), out_local.astype(jnp.bfloat16)], axis=1
    ).reshape(experts, -1, 4 * local_width)
    small_grads = jnp.concatenate([gain_one_grad[None], gain_two_grad[None], router_local], axis=0)
    small_grads = small_grads.reshape(small_grads.shape[0], experts, -1).transpose(1, 0, 2)
    grads_all = reduce_pairs(grads, 6)
    small_grads_all, bias_all = exchange("expert", 4, (small_grads,), (bias_local.T,))
    grads_sum = jnp.sum(grads_all.astype(jnp.float32), axis=0)
    small_sum = jnp.sum(small_grads_all, axis=0)
    qkv_grad = jnp.stack(
        [grads_sum[:, c * local_width : (c + 1) * local_width] for c in range(3)]
    )
    out_grad = grads_sum[:, 3 * local_width :]
    norm1_grad, norm2_grad, router_grad = small_sum[0], small_sum[1], small_sum[2:].T
    bias_grad = jnp.sum(bias_all, axis=0).T
    return (
        block_out,
        input_grad,
        qkv_grad,
        out_grad,
        norm1_grad,
        norm2_grad,
        router_grad,
        bias_grad,
        expert_in_local[None],
        expert_out_local[None],
    )


def solution(mesh):
    placed = (
        P("expert", None),
        P(None, "expert", "shard"),
        P("expert", "shard"),
        P("expert"),
        P("expert"),
        P("expert", None),
        P(None, "shard"),
        P("expert", None, "shard"),
        P("expert", "shard", None),
        P("expert", None),
        P("expert", None),
    )
    return jax.shard_map(
        local,
        mesh=mesh,
        in_specs=placed,
        out_specs=(
            P("expert", None),
            P("expert", None),
            P(None, "expert", "shard"),
            P("expert", "shard"),
            P("expert"),
            P("expert"),
            P("expert", None),
            P(None, "shard"),
            P("expert", None, "shard"),
            P("expert", "shard", None),
        ),
        check_vma=False,
    )
```
